32 devices in a mesh: chan: 8 (over z, y), seg: 4 (over x, core).
Axes of the slice: x: 2, y: 2, z: 4, core: 2. Of those that a mesh axis runs over, the one named last changes fastest.
Arguments:
- traces: bfloat16 [1024, 8192], P('chan', 'seg'), may hold values from -36 to 36
- pair_bins: int32 [2, 1024, 128], P(None, 'chan'), may hold values from 0 to 255
Outputs:
- correlograms: float32 [65, 256], P(None, 'chan')
The draws below stay inside these ranges and needn't reach their ends.
All inputs are finite; a program needn't handle non-finite values.
Results may differ from the reference program's by a relative error of at most 0.0029.
Values may be sent and summed in bfloat16 or wider, within the bound.
A program may use at most 64 MiB of HBM per device.

```python
import math
import jax
import jax.numpy as jnp
from jax import lax

CB = 128
SEG_LEN = 2048
MAX_LAG = 32
NB = 256
ROUNDS = 2
LAGS = 65
CHANNELS = 1024
TIME = 8192
PAIRS_BIN = 1024
N_CHAN = 8
N_SEG = 4


def draw_traces(key, part):
    key_gain = jax.random.fold_in(key, 11)
    key_noise = jax.random.fold_in(key, 12)
    position = jnp.arange(TIME, dtype=jnp.float32) / (TIME - 1)
    gains = jnp.exp(jax.random.uniform(key_gain, (CHANNELS, 1), jnp.float32, math.log(0.3), math.log(3.0)))
    noise = jax.random.truncated_normal(key_noise, -4.0, 4.0, (CHANNELS, TIME), jnp.float32)
    envelope = 1.0 + 2.0 * position
    return (gains * envelope[None, :] * noise).astype(jnp.bfloat16)


def place_ends(drawn, rng, least, top_value):
    index_at = [jax.random.randint(jax.random.fold_in(rng, axis), (), 0, length) for axis, length in enumerate(drawn.shape)]
    widest = drawn.shape.index(max(drawn.shape))
    neighbour = index_at[:widest] + [(index_at[widest] + 1) % drawn.shape[widest]] + index_at[widest + 1:]
    return drawn.at[tuple(index_at)].set(least).at[tuple(neighbour)].set(top_value)


def setup_inputs(seed: int = 0) -> dict:
    key_list = jax.random.split(jax.random.key(seed), 3)
    traces = draw_traces(jax.random.fold_in(key_list[2], 71), 0)
    pair_bins = place_ends(jax.random.randint(key_list[1], (ROUNDS, CHANNELS, CB), 0, NB), jax.random.fold_in(key_list[1], 1), 0, NB - 1).astype(jnp.int32)
    return dict(traces=traces, pair_bins=pair_bins)


EPSILON = 1e-06

def segment_bins(own_block, partner, own_scale, partner_scale, round_bins):
    padded = jnp.pad(partner.astype(jnp.float32), ((0, 0), (MAX_LAG, MAX_LAG)))
    offsets = jnp.arange(LAGS, dtype=jnp.int32)
    shifted = jax.vmap(lambda offset: lax.dynamic_slice_in_dim(padded, offset, SEG_LEN, 1))(offsets)
    raw_sums = jnp.einsum('at,lbt->alb', own_block.astype(jnp.float32), shifted)
    zscore = raw_sums * own_scale[:, None, None] * partner_scale[None, None, :] * (1.0 / math.sqrt(TIME))
    rounded = lax.optimization_barrier(zscore.astype(jnp.bfloat16)).astype(jnp.float32)
    bin_ids = jnp.arange(NB, dtype=jnp.int32)
    onehot = (round_bins[:, :, None] == bin_ids[None, None, :]).astype(jnp.float32)
    return jnp.einsum('alb,abn->ln', rounded, onehot)

def reference(traces, pair_bins):
    squares = lax.optimization_barrier(jnp.sum(jnp.square(traces.astype(jnp.float32)), axis=1))
    inv_rms = lax.rsqrt(squares / TIME + EPSILON)
    blocks = traces.reshape(N_CHAN, CB, N_SEG, SEG_LEN)
    scales = inv_rms.reshape(N_CHAN, CB)
    bin_blocks = pair_bins.reshape(ROUNDS, N_CHAN, CB, CB)
    total = jnp.zeros((LAGS, NB), jnp.float32)
    for round_index in range(ROUNDS):
        distance = N_CHAN // 2 - round_index

        def step_pair(carry, flat_index):
            block_index = flat_index // N_SEG
            segment = flat_index % N_SEG
            partner_index = (block_index + distance) % N_CHAN
            own_block = blocks[block_index, :, segment, :]
            partner = blocks[partner_index, :, segment, :]
            term = segment_bins(own_block, partner, scales[block_index], scales[partner_index], bin_blocks[round_index, block_index])
            return (carry + term, None)
        total, _ = lax.scan(step_pair, total, jnp.arange(N_CHAN * N_SEG, dtype=jnp.int32))
    return total * (1.0 / math.sqrt(PAIRS_BIN))
```

```python
import functools
import math

import jax
import jax.numpy as jnp
from jax import lax
from jax.experimental import pallas as pl
from jax.experimental.pallas import tpu as pltpu
from jax.sharding import PartitionSpec as P

MAX_LAG = 32
NB = 256
ROUNDS = 2
LAGS = 2 * MAX_LAG + 1
EPSILON = 1e-06

FINE = 8
COARSE = 2 * MAX_LAG // FINE
LANES = 128
ROWS = 80
MESH = pl.DeviceIdType.MESH
CONTRACT = (((1,), (1,)), ((), ()))
F32, BF16 = jnp.float32, jnp.bfloat16


def dot(left, right):
    return lax.dot_general(left, right, CONTRACT, preferred_element_type=F32)


def lane_mask(rows, low, high):
    lane = lax.broadcasted_iota(jnp.int32, (rows, LANES), 1)
    return jnp.where((lane >= low) & (lane < high), 1.0, 0.0).astype(BF16)


def near_shifts(source, shifted):
    rows, length = source.shape
    block = source[...]
    for k in range(COARSE):
        step = FINE * (k - COARSE // 2)
        at = slice(k * rows, (k + 1) * rows)
        if step == 0:
            shifted[at, :] = block
            continue
        turned = pltpu.roll(block, step % length, 1)
        if step > 0:
            shifted[at, :LANES] = turned[:, :LANES] * lane_mask(rows, step, LANES)
            shifted[at, LANES:] = turned[:, LANES:]
        else:
            keep = 1 - lane_mask(rows, LANES + step, LANES - FINE)
            shifted[at, : length - LANES] = turned[:, : length - LANES]
            shifted[at, length - LANES :] = turned[:, length - LANES :] * keep


def centre_shifts(block, fine):
    rows, length = block.shape
    for f in range(FINE + 1):
        at = slice(f * rows, (f + 1) * rows)
        if f == 0:
            fine[at, :length] = block
            fine[at, length:] = block[:, length - LANES :] * lane_mask(rows, 0, LANES - FINE)
            continue
        turned = pltpu.roll(block, length - f, 1)
        tail = turned[:, length - LANES :]
        fine[at, : length - LANES] = turned[:, : length - LANES]
        fine[at, length - LANES : length] = tail * lane_mask(rows, 0, LANES - f)
        if f < FINE:
            fine[at, length:] = tail * (1 - lane_mask(rows, LANES - FINE, LANES - f))


def correlate(fine, near, raw):
    width = near.shape[0] // COARSE
    length = near.shape[1]
    total = fine.shape[0]
    rows = total // (FINE + 1)
    plain = FINE * rows
    wrapped = jnp.concatenate([fine[:plain, : length - LANES], fine[:plain, length:]], 1)
    half = COARSE // 2
    spans = ((0, half, wrapped), (half, COARSE - 2, fine[:plain, :length]), (COARSE - 2, COARSE, fine[:, :length]))
    for low, high, left in spans:
        out = dot(left, near[low * width : high * width, :])
        for k in range(low, high):
            raw[k, : left.shape[0], :] = out[:, (k - low) * width : (k - low + 1) * width]


def score(raw, factor, z):
    rows = factor.shape[0]
    width = factor.shape[1]
    for x in range(rows):
        each = jnp.broadcast_to(factor[x : x + 1, :], (FINE, width))
        pieces = [raw[k, pl.ds(x, FINE, stride=rows), :] * each for k in range(COARSE)]
        last = raw[COARSE - 1, pl.ds(FINE * rows + x, 1), :]
        edge = jnp.broadcast_to(last, (FINE, width)) * each
        z[:, x * width : (x + 1) * width] = jnp.concatenate(pieces + [edge, edge], 0).astype(BF16)


def gather_bins(z, table, acc):
    rows, width = table.shape
    ids = lax.broadcasted_iota(jnp.int32, (NB, width), 0).astype(F32)
    hots = []
    for x in range(rows):
        hit = jnp.broadcast_to(table[x : x + 1, :], (NB, width)) == ids
        hots.append(jnp.where(hit, 1.0, 0.0).astype(BF16))
    acc[...] += dot(jnp.concatenate(hots, 1), z[...])


def kernel(
    n_chan, n_seg, x_ref, b_ref, o_ref,
    cbuf, xbuf, nbuf, near_c, near_n, fine, raw, z, e_out, e_in, b_out, b_cross, b_near,
    t_fwd, t_rev, t_two, f_one, f_two, acc_fwd, acc_rev, acc_two, part, arrived, mine, others,
    e_send, e_recv, c_sem, x_send, x_recv, w_send, w_recv, n_send, n_recv, b_send, b_recv, r_send, r_recv, s_send, s_recv,
):
    channels, length = x_ref.shape
    half = channels // 2
    size = half // 2
    chan, seg = lax.axis_index("chan"), lax.axis_index("seg")
    loop = n_chan // 2
    side = chan // loop
    q = chan - side * loop
    parity = lax.rem(seg, 2)
    twin = seg + 1 - 2 * parity
    holder = parity == side
    helper = parity != side
    across = lax.rem(chan + loop, n_chan)
    above = side * loop + lax.rem(q + 1, loop)
    below = side * loop + lax.rem(q + loop - 1, loop)
    base = pl.multiple_of(half * jnp.where(holder, 1, 0), size)
    other_base = pl.multiple_of(half - base, size)
    wrap = (holder & (q == 0)) | (helper & (q == loop - 1))

    def send(src, dst, s_sem, r_sem, device):
        return pltpu.make_async_remote_copy(
            src_ref=src, dst_ref=dst, send_sem=s_sem, recv_sem=r_sem, device_id=device, device_id_type=MESH
        )

    barrier = pltpu.get_barrier_semaphore()
    peers = [(lax.rem(chan + k, n_chan), seg) for k in range(1, n_chan)]
    for k in range(1, n_seg):
        to = lax.rem(seg + k, n_seg)
        peers += [(chan, to), (across, to), (above, to), (below, to)]
    for peer in peers:
        pl.semaphore_signal(barrier, inc=1, device_id=peer, device_id_type=MESH)

    squares = jnp.zeros((channels, LANES), F32)
    for t in range(0, length, LANES):
        squares += jnp.square(x_ref[:, t : t + LANES].astype(F32))
    own_energy = jnp.sum(squares.T, axis=0, keepdims=True)
    e_out[...] = own_energy
    e_in[0, seg] = own_energy
    b_out[...] = b_ref[...].astype(F32).astype(BF16)
    t_fwd[...] = b_ref[0].astype(F32).T

    @pl.when(holder)
    def _():
        near_shifts(x_ref, near_c)

    acc_fwd[...] = jnp.zeros_like(acc_fwd)
    acc_rev[...] = jnp.zeros_like(acc_rev)
    acc_two[...] = jnp.zeros_like(acc_two)
    pl.semaphore_wait(barrier, len(peers))

    e_copies = []
    for k in range(1, n_seg):
        to = lax.rem(seg + k, n_seg)
        e_copies.append(send(e_out, e_in.at[0, seg], e_send.at[0, k], e_recv.at[0, k], (chan, to)))
    for k in range(n_seg):
        to = lax.rem(seg + k, n_seg)
        e_copies.append(send(e_out, e_in.at[1, seg], e_send.at[1, k], e_recv.at[1, k], (across, to)))
    for k in range(n_seg // 2):
        to = lax.rem(2 * k + side + seg - parity, n_seg)
        to_helper = lax.rem(2 * k + 1 - side + seg - parity, n_seg)
        e_copies.append(send(e_out, e_in.at[2, seg], e_send.at[2, k], e_recv.at[2, 2 * k + parity], (above, to)))
        e_copies.append(send(e_out, e_in.at[2, seg], e_send.at[3, k], e_recv.at[2, 2 * k + parity], (below, to_helper)))
    for copy in e_copies:
        copy.start()

    def cross_rows(start):
        return pl.ds(pl.multiple_of(start, size), size)

    def cross(i, to_holder):
        rows = cross_rows(i * size + (half if to_holder else 0))
        return send(x_ref.at[rows], xbuf.at[rows], x_send.at[i, to_holder], x_recv.at[i], (across, seg if to_holder else twin))

    to_twin = send(x_ref, cbuf, c_sem.at[0], c_sem.at[1], (chan, twin))
    to_above = send(x_ref, nbuf, n_send.at[0], n_recv.at[0], (above, seg))
    to_below = send(x_ref, nbuf, n_send.at[1], n_recv.at[0], (below, twin))
    to_wrap = send(x_ref, nbuf, n_send.at[1], n_recv.at[0], (below, seg))
    bins_zero = send(b_out.at[0, pl.ds(0, half)], b_cross, b_send.at[0], b_recv.at[0], (across, seg))
    bins_half = send(b_out.at[0, pl.ds(half, half)], b_cross, b_send.at[1], b_recv.at[0], (across, twin))
    bins_one = send(b_out.at[1], b_near, b_send.at[2], b_recv.at[1], (across, twin))
    bins_below = send(b_out.at[1], b_near, b_send.at[3], b_recv.at[1], (below, twin))
    from_holder = (to_twin, to_above, bins_zero, bins_half, bins_one, bins_below)

    @pl.when(holder)
    def _():
        to_twin.start()
        for copy in (bins_zero, bins_half, bins_one, bins_below):
            copy.start()
        to_above.start()

        @pl.when(q != 0)
        def _():
            to_below.start()

    @pl.when(helper)
    def _():
        for i in range(2):
            cross(i, 1).start()
            cross(i, 0).start()

        @pl.when(q == 0)
        def _():
            to_wrap.start()

        to_twin.wait_recv()
        near_shifts(cbuf, near_c)

    for k in range(1, n_seg):
        send(e_out, e_in.at[0, 0], e_send.at[0, k], e_recv.at[0, k], (chan, seg)).wait_recv()
    for k in range(n_seg):
        send(e_out, e_in.at[1, 0], e_send.at[1, k], e_recv.at[1, k], (chan, seg)).wait_recv()
        send(e_out, e_in.at[2, 0], e_send.at[2, 0], e_recv.at[2, k], (chan, seg)).wait_recv()
    total_time = length * n_seg

    def scale(slot):
        energy = e_in[slot, 0]
        for s in range(1, n_seg):
            energy = energy + e_in[slot, s]
        return lax.rsqrt(energy * (1.0 / total_time) + EPSILON)

    own, cross_scale, next_scale = scale(0), scale(1), scale(2)
    time_scale = 1.0 / math.sqrt(total_time)
    cross_column = jnp.broadcast_to(cross_scale, (channels, channels)).T
    f_one[...] = cross_column * own * time_scale
    centre_scale = jnp.where(wrap, own, cross_scale)
    f_two[...] = jnp.broadcast_to(centre_scale, (channels, channels)).T * next_scale * time_scale
    for copy in (bins_zero, bins_one):
        copy.wait_recv()
    t_rev[...] = b_cross[...].astype(F32)

    @pl.when(helper)
    def _():
        t_two[...] = b_near[...].astype(F32).T

    @pl.when(holder & (q != 0))
    def _():
        t_two[...] = b_near[...].astype(F32)

    @pl.when(holder & (q == 0))
    def _():
        t_two[...] = b_ref[1].astype(F32)

    def forward(i, start):
        rows = cross_rows(start + i * size)
        return send(xbuf.at[rows], xbuf.at[rows], w_send.at[i], w_recv.at[i], (chan, twin))

    for i in range(2):
        rows = cross_rows(base + i * size)
        cross(i, 1).wait_recv()
        forward(i, base).start()
        centre_shifts(xbuf[rows, :], fine)
        correlate(fine, near_c, raw)
        score(raw, f_one[rows, :], z)
        gather_bins(z, t_fwd[rows, :], acc_fwd)
        gather_bins(z, t_rev[pl.ds(i * size, size), :], acc_rev)

    to_above.wait_recv()
    near_shifts(nbuf, near_n)
    for i in range(4):
        start = (base if i < 2 else other_base) + (i % 2) * size
        rows = cross_rows(start)
        if i >= 2:
            forward(i - 2, base).wait_recv()

        @pl.when(wrap)
        def _():
            centre_shifts(x_ref[rows, :], fine)

        @pl.when(jnp.logical_not(wrap))
        def _():
            centre_shifts(xbuf[rows, :], fine)

        correlate(fine, near_n, raw)
        score(raw, f_two[rows, :], z)
        gather_bins(z, t_two[rows, :], acc_two)

    flip = lax.broadcasted_iota(jnp.int32, (ROWS, ROWS), 0) + lax.broadcasted_iota(jnp.int32, (ROWS, ROWS), 1)
    flip = jnp.where(flip == 2 * MAX_LAG, 1.0, 0.0).astype(F32)
    two = acc_two[...]
    ahead = acc_fwd[...] + jnp.where(holder, 0.0, two)
    back = acc_rev[...] + jnp.where(holder, two, 0.0)
    turned = lax.dot_general(
        back, flip, (((1,), (0,)), ((), ())), precision=lax.Precision.HIGHEST, preferred_element_type=F32
    )
    pair_total = ROUNDS * n_chan * channels * channels // NB
    part[...] = jnp.zeros_like(part)
    part[:, :ROWS] = (ahead + turned) * (1.0 / math.sqrt(pair_total))

    owned = part.shape[0] // n_chan
    first = []
    for k in range(1, n_chan):
        peer = lax.rem(chan + k, n_chan)
        src = part.at[pl.ds(pl.multiple_of(peer * owned, owned), owned)]
        copy = send(src, arrived.at[k - 1], r_send.at[k - 1], r_recv.at[k - 1], (peer, seg))
        copy.start()
        first.append(copy)
    running = part[pl.ds(pl.multiple_of(chan * owned, owned), owned), :]
    for k, copy in enumerate(first):
        copy.wait_recv()
        running = running + arrived[k]
    mine[...] = running
    others[seg] = running
    second = []
    for k in range(1, n_seg):
        copy = send(mine, others.at[seg], s_send.at[k], s_recv.at[k], (chan, lax.rem(seg + k, n_seg)))
        copy.start()
        second.append(copy)
    for copy in second:
        copy.wait_recv()
    sums = others[0]
    for s in range(1, n_seg):
        sums = sums + others[s]
    o_ref[...] = sums.T[:LAGS, :]

    for copy in e_copies + first + second:
        copy.wait_send()
    for i in range(2):
        forward(i, base).wait_send()

    @pl.when(holder)
    def _():
        for copy in from_holder:
            copy.wait_send()

        @pl.when(q != 0)
        def _():
            to_below.wait_send()

    @pl.when(helper)
    def _():
        for i in range(2):
            cross(i, 1).wait_send()
            cross(i, 0).wait_send()

        @pl.when(q == 0)
        def _():
            to_wrap.wait_send()


def local(traces, pair_bins):
    channels, length = traces.shape
    n_chan, n_seg = lax.axis_size("chan"), lax.axis_size("seg")
    size = channels // 4
    owned = NB // n_chan
    dma = pltpu.SemaphoreType.DMA
    block = pltpu.VMEM((channels, length), BF16)
    square = pltpu.VMEM((channels, channels), F32)
    stacked = pltpu.VMEM((NB, ROWS), F32)
    return pl.pallas_call(
        functools.partial(kernel, n_chan, n_seg),
        out_shape=jax.ShapeDtypeStruct((LAGS, owned), F32),
        in_specs=[pl.BlockSpec(memory_space=pltpu.VMEM)] * 2,
        out_specs=pl.BlockSpec(memory_space=pltpu.VMEM),
        scratch_shapes=[
            block, block, block,
            pltpu.VMEM((COARSE * channels, length), BF16),
            pltpu.VMEM((COARSE * channels, length), BF16),
            pltpu.VMEM(((FINE + 1) * size, length + LANES), BF16),
            pltpu.VMEM((COARSE, (FINE + 1) * size, channels), F32),
            pltpu.VMEM((ROWS, size * channels), BF16),
            pltpu.VMEM((1, channels), F32),
            pltpu.VMEM((3, n_seg, 1, channels), F32),
            pltpu.VMEM((2, channels, channels), BF16),
            pltpu.VMEM((channels // 2, channels), BF16),
            pltpu.VMEM((channels, channels), BF16),
            square, pltpu.VMEM((channels // 2, channels), F32), square, square, square,
            stacked, stacked, stacked,
            pltpu.VMEM((NB, LANES), F32),
            pltpu.VMEM((n_chan - 1, owned, LANES), F32),
            pltpu.VMEM((owned, LANES), F32),
            pltpu.VMEM((n_seg, owned, LANES), F32),
            dma((4, n_seg)), dma((3, n_seg)), dma((2,)), dma((2, 2)), dma((2,)), dma((2,)), dma((2,)),
            dma((2,)), dma((1,)), dma((4,)), dma((2,)),
            dma((n_chan - 1,)), dma((n_chan - 1,)), dma((n_seg,)), dma((n_seg,)),
        ],
        compiler_params=pltpu.CompilerParams(
            collective_id=0, has_side_effects=True, vmem_limit_bytes=48 * 1024 * 1024
        ),
    )(traces, pair_bins)


def solution(mesh):
    in_specs = (P("chan", "seg"), P(None, "chan", None))
    out_specs = P(None, "chan")
    return jax.shard_map(local, mesh=mesh, in_specs=in_specs, out_specs=out_specs, check_vma=False)
```

```python
import functools
import math

import jax
import jax.numpy as jnp
from jax import lax
from jax.experimental import pallas as pl
from jax.experimental.pallas import tpu as pltpu
from jax.sharding import PartitionSpec as P

MAX_LAG = 32
NB = 256
ROUNDS = 2
LAGS = 2 * MAX_LAG + 1
EPSILON = 1e-06

FINE = 8
COARSE = 2 * MAX_LAG // FINE
LANES = 128
ROWS = 80
TILE = 16
GROUP = 8
MESH = pl.DeviceIdType.MESH
CONTRACT = (((1,), (1,)), ((), ()))
F32, BF16 = jnp.float32, jnp.bfloat16

NEAR = MAX_LAG - FINE
SPAN = FINE


def dot(left, right):
    return lax.dot_general(left, right, CONTRACT, preferred_element_type=F32)


def lanes(rows):
    return lax.broadcasted_iota(jnp.int32, (rows, LANES), 1)


def columns_first(cols):
    count = len(cols)
    lane = lanes(cols[0].shape[0])
    step = 1
    while step < count:
        bit = (lane & step) != 0
        done = list(cols)
        for u in range(count):
            if not u & step:
                low, high = cols[u], cols[u + step]
                done[u] = jnp.where(bit, pltpu.roll(high, step, 1), low)
                done[u + step] = jnp.where(bit, high, pltpu.roll(low, LANES - step, 1))
        cols = done
        step *= 2
    return cols


def later(col, count):
    lane = lanes(col.shape[0])
    inner = pltpu.roll(col, LANES - count, 1)
    outer = jnp.where(lane < LANES - 1, pltpu.roll(col, LANES - count - 1, 1), 0.0)
    return jnp.where(lane < LANES - count, inner, outer)


def earlier(col, count):
    lane = lanes(col.shape[0])
    inner = pltpu.roll(col, count, 1)
    outer = jnp.where(lane > 0, pltpu.roll(col, count + 1, 1), 0.0)
    return jnp.where(lane >= count, inner, outer)


def at(column):
    return slice(column * LANES, (column + 1) * LANES)


def beside(load, store, count, low, high):
    for i in range(count):
        col = None
        for c in range(i + count, count + high, count):
            col = later(load(i) if col is None else col, count)
            store(c, col)
        col = None
        for c in range(i - count, -low - 1, -count):
            col = earlier(load(i) if col is None else col, count)
            store(c, col)


def spread_near(source, wide):
    rows, length = source.shape
    count = length // LANES

    @pl.loop(0, rows // TILE)
    def _(g):
        here = pl.ds(pl.multiple_of(g * TILE, TILE), TILE)
        wide[here, NEAR * LANES : NEAR * LANES + length] = source[here, :]

        def store(c, col):
            wide[here, at(NEAR + c)] = col.astype(BF16)

        beside(lambda i: source[here, at(i)].astype(F32), store, count, NEAR, NEAR)


def spread_centre(block, start, rows, count):
    @pl.loop(0, rows // TILE)
    def _(g):
        here = pl.ds(pl.multiple_of(start + g * TILE, TILE), TILE)

        def store(c, col):
            block[here, at(SPAN + c)] = col.astype(BF16)

        beside(lambda i: block[here, at(SPAN + i)].astype(F32), store, count, SPAN, SPAN)


def correlate(centre, near, raw, piece):
    rows, span = centre.shape
    length = span - 2 * SPAN * LANES
    pair = 2
    steps = FINE + 1 if piece == COARSE // pair - 1 else FINE
    first = 0 if piece < COARSE // pair // 2 else SPAN
    left = [centre[:, (first + f) * LANES : (first + f) * LANES + length] for f in range(steps)]
    right = []
    for k in range(pair * piece, pair * piece + pair):
        column = NEAR - FINE * (k - COARSE // 2) - (FINE if k < COARSE // 2 else 0)
        right.append(near[:, column * LANES : column * LANES + length])
    out = dot(jnp.concatenate(left, 0), jnp.concatenate(right, 0))
    width = near.shape[0]
    for k in range(pair):
        raw[pair * piece + k, : steps * rows, :] = out[:, k * width : (k + 1) * width]


def bin_rows(raw, rows, group, factor, targets):
    width = factor.shape[1]
    scores = []
    for x in range(group * GROUP, (group + 1) * GROUP):
        each = jnp.broadcast_to(factor[x : x + 1, :], (FINE, width))
        pieces = [raw[k, pl.ds(x, FINE, stride=rows), :] * each for k in range(COARSE)]
        last = raw[COARSE - 1, pl.ds(FINE * rows + x, 1), :]
        edge = jnp.broadcast_to(last, (FINE, width)) * each
        scores.append(jnp.concatenate(pieces + [edge, edge], 0).astype(BF16))
    score = jnp.concatenate(scores, 1)
    ids = lax.broadcasted_iota(jnp.int32, (NB, width), 0).astype(F32).astype(BF16)
    one, none = jnp.asarray(1, BF16), jnp.asarray(0, BF16)
    for table, acc in targets:
        hots = []
        for x in range(group * GROUP, (group + 1) * GROUP):
            hit = jnp.broadcast_to(table[x : x + 1, :].astype(BF16), (NB, width)) == ids
            hots.append(jnp.where(hit, one, none))
        acc[...] += dot(jnp.concatenate(hots, 1), score)


def kernel(
    n_chan, n_seg, x_ref, b_ref, o_ref,
    trace, bins, cbuf, centres, nbuf, near_c, near_n, raw, i_sem, e_out, e_in, b_out, b_cross, b_near,
    t_fwd, t_rev, t_two, f_one, f_two, acc_fwd, acc_rev, acc_two, squares, part, arrived, mine, others,
    e_send, e_recv, c_sem, x_send, x_recv, w_send, w_recv, n_send, n_recv, b_send, b_recv, r_send, r_recv, s_send, s_recv,
):
    channels, length = trace.shape
    count = length // LANES
    half = channels // 2
    size = half // 2
    chan, seg = lax.axis_index("chan"), lax.axis_index("seg")
    loop = n_chan // 2
    side = chan // loop
    q = chan - side * loop
    parity = lax.rem(seg, 2)
    twin = seg + 1 - 2 * parity
    holder = parity == side
    helper = parity != side
    across = lax.rem(chan + loop, n_chan)
    above = side * loop + lax.rem(q + 1, loop)
    below = side * loop + lax.rem(q + loop - 1, loop)
    base = pl.multiple_of(half * jnp.where(holder, 1, 0), size)
    other_base = pl.multiple_of(half - base, size)
    wrap = (holder & (q == 0)) | (helper & (q == loop - 1))

    def send(src, dst, s_sem, r_sem, device):
        return pltpu.make_async_remote_copy(
            src_ref=src, dst_ref=dst, send_sem=s_sem, recv_sem=r_sem, device_id=device, device_id_type=MESH
        )

    bins_in = pltpu.make_async_copy(b_ref, bins, i_sem.at[0])
    trace_in = pltpu.make_async_copy(x_ref, trace, i_sem.at[1])
    trace_in.start()
    bins_in.start()
    xbuf = centres.at[0, :, pl.ds(SPAN * LANES, length)]
    own = centres.at[1, :, pl.ds(SPAN * LANES, length)]
    barrier = pltpu.get_barrier_semaphore()
    peers = [(lax.rem(chan + k, n_chan), seg) for k in range(1, n_chan)]
    for k in range(1, n_seg):
        to = lax.rem(seg + k, n_seg)
        peers += [(chan, to), (across, to), (above, to), (below, to)]
    for peer in peers:
        pl.semaphore_signal(barrier, inc=1, device_id=peer, device_id_type=MESH)

    bins_in.wait()
    b_out[...] = bins[...].astype(F32).astype(BF16)
    t_fwd[...] = bins[0].astype(F32).T
    trace_in.wait()
    squares[...] = jnp.zeros_like(squares)

    @pl.loop(0, channels // TILE)
    def _(g):
        here = pl.ds(pl.multiple_of(g * TILE, TILE), TILE)
        cols = [trace[here, at(i)].astype(F32) for i in range(count)]
        total = jnp.square(cols[0])
        for col in cols[1:]:
            total += jnp.square(col)
        squares[here, :] = total
        for i, col in enumerate(columns_first(cols)):
            own[here, at(i)] = col.astype(BF16)

    own_energy = jnp.sum(squares[...].T, axis=0, keepdims=True)
    e_out[...] = own_energy
    e_in[0, seg] = own_energy
    acc_fwd[...] = jnp.zeros_like(acc_fwd)
    acc_rev[...] = jnp.zeros_like(acc_rev)
    acc_two[...] = jnp.zeros_like(acc_two)
    pl.semaphore_wait(barrier, len(peers))

    e_copies = []
    for k in range(1, n_seg):
        to = lax.rem(seg + k, n_seg)
        e_copies.append(send(e_out, e_in.at[0, seg], e_send.at[0, k], e_recv.at[0, k], (chan, to)))
    for k in range(n_seg):
        to = lax.rem(seg + k, n_seg)
        e_copies.append(send(e_out, e_in.at[1, seg], e_send.at[1, k], e_recv.at[1, k], (across, to)))
    for k in range(n_seg // 2):
        to = lax.rem(2 * k + side + seg - parity, n_seg)
        to_helper = lax.rem(2 * k + 1 - side + seg - parity, n_seg)
        e_copies.append(send(e_out, e_in.at[2, seg], e_send.at[2, k], e_recv.at[2, 2 * k + parity], (above, to)))
        e_copies.append(send(e_out, e_in.at[2, seg], e_send.at[3, k], e_recv.at[2, 2 * k + parity], (below, to_helper)))
    for copy in e_copies:
        copy.start()

    def cross_rows(start):
        return pl.ds(pl.multiple_of(start, size), size)

    def cross(i, to_holder):
        rows = cross_rows(i * size + (half if to_holder else 0))
        return send(own.at[rows], xbuf.at[rows], x_send.at[i, to_holder], x_recv.at[i], (across, seg if to_holder else twin))

    to_twin = send(own, cbuf, c_sem.at[0], c_sem.at[1], (chan, twin))
    to_above = send(own, nbuf, n_send.at[0], n_recv.at[0], (above, seg))
    to_below = send(own, nbuf, n_send.at[1], n_recv.at[0], (below, twin))
    to_wrap = send(own, nbuf, n_send.at[1], n_recv.at[0], (below, seg))
    bins_zero = send(b_out.at[0, pl.ds(0, half)], b_cross, b_send.at[0], b_recv.at[0], (across, seg))
    bins_half = send(b_out.at[0, pl.ds(half, half)], b_cross, b_send.at[1], b_recv.at[0], (across, twin))
    bins_one = send(b_out.at[1], b_near, b_send.at[2], b_recv.at[1], (across, twin))
    bins_below = send(b_out.at[1], b_near, b_send.at[3], b_recv.at[1], (below, twin))
    from_holder = (to_twin, to_above, bins_zero, bins_half, bins_one, bins_below)

    @pl.when(holder)
    def _():
        to_twin.start()
        for copy in (bins_zero, bins_half, bins_one, bins_below):
            copy.start()
        to_above.start()

        @pl.when(q != 0)
        def _():
            to_below.start()

        spread_near(own, near_c)

    @pl.when(helper)
    def _():
        for i in range(2):
            cross(i, 1).start()
            cross(i, 0).start()

        @pl.when(q == 0)
        def _():
            to_wrap.start()

        to_twin.wait_recv()
        spread_near(cbuf, near_c)

    for k in range(1, n_seg):
        send(e_out, e_in.at[0, 0], e_send.at[0, k], e_recv.at[0, k], (chan, seg)).wait_recv()
    for k in range(n_seg):
        send(e_out, e_in.at[1, 0], e_send.at[1, k], e_recv.at[1, k], (chan, seg)).wait_recv()
        send(e_out, e_in.at[2, 0], e_send.at[2, 0], e_recv.at[2, k], (chan, seg)).wait_recv()
    total_time = length * n_seg

    def scale(slot):
        energy = e_in[slot, 0]
        for s in range(1, n_seg):
            energy = energy + e_in[slot, s]
        return lax.rsqrt(energy * (1.0 / total_time) + EPSILON)

    own_scale, cross_scale, next_scale = scale(0), scale(1), scale(2)
    time_scale = 1.0 / math.sqrt(total_time)
    cross_column = jnp.broadcast_to(cross_scale, (channels, channels)).T
    f_one[...] = cross_column * own_scale * time_scale
    centre_scale = jnp.where(wrap, own_scale, cross_scale)
    f_two[...] = jnp.broadcast_to(centre_scale, (channels, channels)).T * next_scale * time_scale
    for copy in (bins_zero, bins_one):
        copy.wait_recv()
    t_rev[...] = b_cross[...].astype(F32)

    @pl.when(helper)
    def _():
        t_two[...] = b_near[...].astype(F32).T

    @pl.when(holder & (q != 0))
    def _():
        t_two[...] = b_near[...].astype(F32)

    @pl.when(holder & (q == 0))
    def _():
        t_two[...] = bins[1].astype(F32)

    def forward(i, start):
        rows = cross_rows(start + i * size)
        return send(xbuf.at[rows], xbuf.at[rows], w_send.at[i], w_recv.at[i], (chan, twin))

    pieces = size // GROUP

    def advance(i, centre, near, after):
        for p in range(pieces):
            if centre is not None:
                correlate(centre, near, raw.at[i % 2], p)
            if after is not None:
                bin_rows(raw.at[(i + 1) % 2], size, p, *after)

    after = None
    for i in range(2):
        rows = cross_rows(base + i * size)
        cross(i, 1).wait_recv()
        forward(i, base).start()
        spread_centre(centres.at[0], base + i * size, size, count)
        advance(i, centres.at[0, rows], near_c, after)
        late = pl.ds(i * size, size)
        after = (f_one.at[rows], ((t_fwd.at[rows], acc_fwd), (t_rev.at[late], acc_rev)))

    @pl.when(wrap)
    def _():
        spread_centre(centres.at[1], 0, channels, count)

    chosen = jnp.where(wrap, 1, 0)
    to_above.wait_recv()
    spread_near(nbuf, near_n)
    for i in range(4):
        start = (base if i < 2 else other_base) + (i % 2) * size
        rows = cross_rows(start)
        if i >= 2:
            forward(i - 2, base).wait_recv()
            spread_centre(centres.at[0], start, size, count)
        advance(i, centres.at[chosen, rows], near_n, after)
        after = (f_two.at[rows], ((t_two.at[rows], acc_two),))
    advance(4, None, None, after)

    flip = lax.broadcasted_iota(jnp.int32, (ROWS, ROWS), 0) + lax.broadcasted_iota(jnp.int32, (ROWS, ROWS), 1)
    flip = jnp.where(flip == 2 * MAX_LAG, 1.0, 0.0).astype(F32)
    two = acc_two[...]
    ahead = acc_fwd[...] + jnp.where(holder, 0.0, two)
    back = acc_rev[...] + jnp.where(holder, two, 0.0)
    turned = lax.dot_general(
        back, flip, (((1,), (0,)), ((), ())), precision=lax.Precision.HIGHEST, preferred_element_type=F32
    )
    pair_total = ROUNDS * n_chan * channels * channels // NB
    part[...] = jnp.zeros_like(part)
    part[:, :ROWS] = (ahead + turned) * (1.0 / math.sqrt(pair_total))

    owned = part.shape[0] // n_chan
    first = []
    for k in range(1, n_chan):
        peer = lax.rem(chan + k, n_chan)
        src = part.at[pl.ds(pl.multiple_of(peer * owned, owned), owned)]
        copy = send(src, arrived.at[k - 1], r_send.at[k - 1], r_recv.at[k - 1], (peer, seg))
        copy.start()
        first.append(copy)
    running = part[pl.ds(pl.multiple_of(chan * owned, owned), owned), :]
    for k, copy in enumerate(first):
        copy.wait_recv()
        running = running + arrived[k]
    mine[...] = running
    others[seg] = running
    second = []
    for k in range(1, n_seg):
        copy = send(mine, others.at[seg], s_send.at[k], s_recv.at[k], (chan, lax.rem(seg + k, n_seg)))
        copy.start()
        second.append(copy)
    for copy in second:
        copy.wait_recv()
    sums = others[0]
    for s in range(1, n_seg):
        sums = sums + others[s]
    o_ref[...] = sums.T[:LAGS, :]

    for copy in e_copies + first + second:
        copy.wait_send()
    for i in range(2):
        forward(i, base).wait_send()

    @pl.when(holder)
    def _():
        for copy in from_holder:
            copy.wait_send()

        @pl.when(q != 0)
        def _():
            to_below.wait_send()

    @pl.when(helper)
    def _():
        for i in range(2):
            cross(i, 1).wait_send()
            cross(i, 0).wait_send()

        @pl.when(q == 0)
        def _():
            to_wrap.wait_send()


def local(traces, pair_bins):
    channels, length = traces.shape
    n_chan, n_seg = lax.axis_size("chan"), lax.axis_size("seg")
    size = channels // 4
    owned = NB // n_chan
    dma = pltpu.SemaphoreType.DMA
    block = pltpu.VMEM((channels, length), BF16)
    square = pltpu.VMEM((channels, channels), F32)
    wide = pltpu.VMEM((channels, length + 2 * NEAR * LANES), BF16)
    stacked = pltpu.VMEM((NB, ROWS), F32)
    return pl.pallas_call(
        functools.partial(kernel, n_chan, n_seg),
        out_shape=jax.ShapeDtypeStruct((LAGS, owned), F32),
        in_specs=[pl.BlockSpec(memory_space=pltpu.HBM)] * 2,
        out_specs=pl.BlockSpec(memory_space=pltpu.VMEM),
        scratch_shapes=[
            block,
            pltpu.VMEM((2, channels, channels), jnp.int32),
            block,
            pltpu.VMEM((2, channels, length + 2 * SPAN * LANES), BF16),
            block, wide, wide,
            pltpu.VMEM((2, COARSE, (FINE + 1) * size, channels), F32),
            dma((2,)),
            pltpu.VMEM((1, channels), F32),
            pltpu.VMEM((3, n_seg, 1, channels), F32),
            pltpu.VMEM((2, channels, channels), BF16),
            pltpu.VMEM((channels // 2, channels), BF16),
            pltpu.VMEM((channels, channels), BF16),
            square, pltpu.VMEM((channels // 2, channels), F32), square, square, square,
            stacked, stacked, stacked,
            pltpu.VMEM((channels, LANES), F32),
            pltpu.VMEM((NB, LANES), F32),
            pltpu.VMEM((n_chan - 1, owned, LANES), F32),
            pltpu.VMEM((owned, LANES), F32),
            pltpu.VMEM((n_seg, owned, LANES), F32),
            dma((4, n_seg)), dma((3, n_seg)), dma((2,)), dma((2, 2)), dma((2,)), dma((2,)), dma((2,)),
            dma((2,)), dma((1,)), dma((4,)), dma((2,)),
            dma((n_chan - 1,)), dma((n_chan - 1,)), dma((n_seg,)), dma((n_seg,)),
        ],
        compiler_params=pltpu.CompilerParams(
            collective_id=0, has_side_effects=True, vmem_limit_bytes=48 * 1024 * 1024
        ),
    )(traces, pair_bins)


def solution(mesh):
    in_specs = (P("chan", "seg"), P(None, "chan", None))
    out_specs = P(None, "chan")
    return jax.shard_map(local, mesh=mesh, in_specs=in_specs, out_specs=out_specs, check_vma=False)
```

```python
import functools
import math

import jax
import jax.numpy as jnp
from jax import lax
from jax.experimental import pallas as pl
from jax.experimental.pallas import tpu as pltpu
from jax.sharding import PartitionSpec as P

MAX_LAG = 32
NB = 256
ROUNDS = 2
LAGS = 2 * MAX_LAG + 1
EPSILON = 1e-06

FINE = 8
COARSE = 2 * MAX_LAG // FINE
LANES = 128
ROWS = 80
TILE = 16
GROUP = 8
MESH = pl.DeviceIdType.MESH
CONTRACT = (((1,), (1,)), ((), ()))
F32, BF16 = jnp.float32, jnp.bfloat16

NEAR = MAX_LAG - FINE
SPAN = FINE


def dot(left, right):
    return lax.dot_general(left, right, CONTRACT, preferred_element_type=F32)


def lanes(rows):
    return lax.broadcasted_iota(jnp.int32, (rows, LANES), 1)


def columns_first(cols):
    count = len(cols)
    lane = lanes(cols[0].shape[0])
    step = 1
    while step < count:
        bit = (lane & step) != 0
        done = list(cols)
        for u in range(count):
            if not u & step:
                low, high = cols[u], cols[u + step]
                done[u] = jnp.where(bit, pltpu.roll(high, step, 1), low)
                done[u + step] = jnp.where(bit, high, pltpu.roll(low, LANES - step, 1))
        cols = done
        step *= 2
    return cols


def later(col, count):
    lane = lanes(col.shape[0])
    inner = pltpu.roll(col, LANES - count, 1)
    outer = jnp.where(lane < LANES - 1, pltpu.roll(col, LANES - count - 1, 1), 0.0)
    return jnp.where(lane < LANES - count, inner, outer)


def earlier(col, count):
    lane = lanes(col.shape[0])
    inner = pltpu.roll(col, count, 1)
    outer = jnp.where(lane > 0, pltpu.roll(col, count + 1, 1), 0.0)
    return jnp.where(lane >= count, inner, outer)


def at(column):
    return slice(column * LANES, (column + 1) * LANES)


def beside(load, store, count, low, high):
    for i in range(count):
        col = None
        for c in range(i + count, count + high, count):
            col = later(load(i) if col is None else col, count)
            store(c, col)
        col = None
        for c in range(i - count, -low - 1, -count):
            col = earlier(load(i) if col is None else col, count)
            store(c, col)


def spread_near(source, wide):
    rows, length = source.shape
    count = length // LANES

    @pl.loop(0, rows // TILE, unroll=True)
    def _(g):
        here = pl.ds(pl.multiple_of(g * TILE, TILE), TILE)
        wide[here, NEAR * LANES : NEAR * LANES + length] = source[here, :]

        def store(c, col):
            wide[here, at(NEAR + c)] = col.astype(BF16)

        beside(lambda i: source[here, at(i)].astype(F32), store, count, NEAR, NEAR)


def spread_centre(block, start, rows, count):
    @pl.loop(0, rows // TILE, unroll=True)
    def _(g):
        here = pl.ds(pl.multiple_of(start + g * TILE, TILE), TILE)

        def store(c, col):
            block[here, at(SPAN + c)] = col.astype(BF16)

        beside(lambda i: block[here, at(SPAN + i)].astype(F32), store, count, SPAN, SPAN)


def correlate(centre, near, raw, piece):
    rows, span = centre.shape
    length = span - 2 * SPAN * LANES
    pair = 2
    steps = FINE + 1 if piece == COARSE // pair - 1 else FINE
    first = 0 if piece < COARSE // pair // 2 else SPAN
    left = [centre[:, (first + f) * LANES : (first + f) * LANES + length] for f in range(steps)]
    right = []
    for k in range(pair * piece, pair * piece + pair):
        column = NEAR - FINE * (k - COARSE // 2) - (FINE if k < COARSE // 2 else 0)
        right.append(near[:, column * LANES : column * LANES + length])
    out = dot(jnp.concatenate(left, 0), jnp.concatenate(right, 0))
    width = near.shape[0]
    for k in range(pair):
        raw[pair * piece + k, : steps * rows, :] = out[:, k * width : (k + 1) * width]


def bin_rows(raw, rows, group, factor, targets):
    width = factor.shape[1]
    scores = []
    for x in range(group * GROUP, (group + 1) * GROUP):
        each = jnp.broadcast_to(factor[x : x + 1, :], (FINE, width))
        pieces = [raw[k, pl.ds(x, FINE, stride=rows), :] * each for k in range(COARSE)]
        last = raw[COARSE - 1, pl.ds(FINE * rows + x, 1), :]
        edge = jnp.broadcast_to(last, (FINE, width)) * each
        scores.append(jnp.concatenate(pieces + [edge, edge], 0).astype(BF16))
    score = jnp.concatenate(scores, 1)
    ids = lax.broadcasted_iota(jnp.int32, (NB, width), 0).astype(F32).astype(BF16)
    one, none = jnp.asarray(1, BF16), jnp.asarray(0, BF16)
    for table, acc in targets:
        hots = []
        for x in range(group * GROUP, (group + 1) * GROUP):
            hit = jnp.broadcast_to(table[x : x + 1, :].astype(BF16), (NB, width)) == ids
            hots.append(jnp.where(hit, one, none))
        acc[...] += dot(jnp.concatenate(hots, 1), score)


def kernel(
    n_chan, n_seg, x_ref, b_ref, o_ref,
    trace, bins, cbuf, centres, nbuf, near_c, near_n, raw, i_sem, e_out, e_in, b_out, b_cross, b_near,
    t_fwd, t_rev, t_two, f_one, f_two, acc_fwd, acc_rev, acc_two, squares, part, arrived, mine, others,
    e_send, e_recv, c_sem, x_send, x_recv, w_send, w_recv, n_send, n_recv, b_send, b_recv, r_send, r_recv, s_send, s_recv, known,
):
    channels, length = trace.shape
    count = length // LANES
    half = channels // 2
    size = half // 2
    chan, seg = lax.axis_index("chan"), lax.axis_index("seg")
    loop = n_chan // 2
    side = chan // loop
    q = chan - side * loop
    parity = lax.rem(seg, 2)
    twin = seg + 1 - 2 * parity
    holder = parity == side
    helper = parity != side
    across = lax.rem(chan + loop, n_chan)
    above = side * loop + lax.rem(q + 1, loop)
    below = side * loop + lax.rem(q + loop - 1, loop)
    base = pl.multiple_of(half * jnp.where(holder, 1, 0), size)
    other_base = pl.multiple_of(half - base, size)
    wrap = (holder & (q == 0)) | (helper & (q == loop - 1))

    def send(src, dst, s_sem, r_sem, device):
        return pltpu.make_async_remote_copy(
            src_ref=src, dst_ref=dst, send_sem=s_sem, recv_sem=r_sem, device_id=device, device_id_type=MESH
        )

    bins_in = pltpu.make_async_copy(b_ref, bins, i_sem.at[0])
    trace_in = pltpu.make_async_copy(x_ref, trace, i_sem.at[1])
    trace_in.start()
    bins_in.start()
    xbuf = centres.at[0, :, pl.ds(SPAN * LANES, length)]
    own = centres.at[1, :, pl.ds(SPAN * LANES, length)]
    barrier = pltpu.get_barrier_semaphore()
    beside_us = [(across, seg), (above, seg), (below, seg)]
    peers = list(beside_us)
    for k in range(1, n_seg):
        to = lax.rem(seg + k, n_seg)
        peers += [(chan, to), (across, to), (above, to), (below, to)]
    for peer in peers:
        pl.semaphore_signal(barrier, inc=1, device_id=peer, device_id_type=MESH)

    bins_in.wait()
    b_out[...] = bins[...].astype(F32).astype(BF16)
    trace_in.wait()
    squares[...] = jnp.zeros_like(squares)

    @pl.loop(0, channels // TILE, unroll=True)
    def _(g):
        here = pl.ds(pl.multiple_of(g * TILE, TILE), TILE)
        cols = [trace[here, at(i)].astype(F32) for i in range(count)]
        total = jnp.square(cols[0])
        for col in cols[1:]:
            total += jnp.square(col)
        squares[here, :] = total
        for i, col in enumerate(columns_first(cols)):
            own[here, at(i)] = col.astype(BF16)

    own_energy = jnp.sum(squares[...].T, axis=0, keepdims=True)
    e_out[...] = own_energy
    e_in[0, seg] = own_energy
    acc_fwd[...] = jnp.zeros_like(acc_fwd)
    acc_rev[...] = jnp.zeros_like(acc_rev)
    acc_two[...] = jnp.zeros_like(acc_two)
    pl.semaphore_wait(barrier, len(peers))

    def tell(i):
        for peer in beside_us:
            pl.semaphore_signal(known.at[i], inc=1, device_id=peer, device_id_type=MESH)

    rounds = loop // 2
    tell(0)

    e_copies = []
    for k in range(1, n_seg):
        to = lax.rem(seg + k, n_seg)
        e_copies.append(send(e_out, e_in.at[0, seg], e_send.at[0, k], e_recv.at[0, k], (chan, to)))
    for k in range(n_seg):
        to = lax.rem(seg + k, n_seg)
        e_copies.append(send(e_out, e_in.at[1, seg], e_send.at[1, k], e_recv.at[1, k], (across, to)))
    for k in range(n_seg // 2):
        to = lax.rem(2 * k + side + seg - parity, n_seg)
        to_helper = lax.rem(2 * k + 1 - side + seg - parity, n_seg)
        e_copies.append(send(e_out, e_in.at[2, seg], e_send.at[2, k], e_recv.at[2, 2 * k + parity], (above, to)))
        e_copies.append(send(e_out, e_in.at[2, seg], e_send.at[3, k], e_recv.at[2, 2 * k + parity], (below, to_helper)))
    for copy in e_copies:
        copy.start()

    def cross_rows(start):
        return pl.ds(pl.multiple_of(start, size), size)

    def cross(i, to_holder):
        rows = cross_rows(i * size + (half if to_holder else 0))
        return send(own.at[rows], xbuf.at[rows], x_send.at[i, to_holder], x_recv.at[i], (across, seg if to_holder else twin))

    to_twin = send(own, cbuf, c_sem.at[0], c_sem.at[1], (chan, twin))
    to_above = send(own, nbuf, n_send.at[0], n_recv.at[0], (above, seg))
    to_below = send(own, nbuf, n_send.at[1], n_recv.at[0], (below, twin))
    to_wrap = send(own, nbuf, n_send.at[1], n_recv.at[0], (below, seg))
    bins_zero = send(b_out.at[0, pl.ds(0, half)], b_cross, b_send.at[0], b_recv.at[0], (across, seg))
    bins_half = send(b_out.at[0, pl.ds(half, half)], b_cross, b_send.at[1], b_recv.at[0], (across, twin))
    bins_one = send(b_out.at[1], b_near, b_send.at[2], b_recv.at[1], (across, twin))
    bins_below = send(b_out.at[1], b_near, b_send.at[3], b_recv.at[1], (below, twin))
    from_holder = (to_twin, to_above, bins_zero, bins_half, bins_one, bins_below)

    @pl.when(holder)
    def _():
        to_twin.start()
        for copy in (bins_zero, bins_half, bins_one, bins_below):
            copy.start()
        to_above.start()

        @pl.when(q != 0)
        def _():
            to_below.start()

        spread_near(own, near_c)

    @pl.when(helper)
    def _():
        for i in range(2):
            cross(i, 1).start()
            cross(i, 0).start()

        @pl.when(q == 0)
        def _():
            to_wrap.start()

        to_twin.wait_recv()
        spread_near(cbuf, near_c)

    def forward(i, start):
        rows = cross_rows(start + i * size)
        return send(xbuf.at[rows], xbuf.at[rows], w_send.at[i], w_recv.at[i], (chan, twin))

    pieces = size // GROUP

    def advance(i, centre, near, after):
        for p in range(pieces):
            if centre is not None:
                correlate(centre, near, raw.at[i % 2], p)
            if after is not None:
                bin_rows(raw.at[(i + 1) % 2], size, p, *after)

    def tables():
        for k in range(1, n_seg):
            send(e_out, e_in.at[0, 0], e_send.at[0, k], e_recv.at[0, k], (chan, seg)).wait_recv()
        for k in range(n_seg):
            send(e_out, e_in.at[1, 0], e_send.at[1, k], e_recv.at[1, k], (chan, seg)).wait_recv()
            send(e_out, e_in.at[2, 0], e_send.at[2, 0], e_recv.at[2, k], (chan, seg)).wait_recv()
        total_time = length * n_seg

        def scale(slot):
            energy = e_in[slot, 0]
            for s in range(1, n_seg):
                energy = energy + e_in[slot, s]
            return lax.rsqrt(energy * (1.0 / total_time) + EPSILON)

        own_scale, cross_scale, next_scale = scale(0), scale(1), scale(2)
        time_scale = 1.0 / math.sqrt(total_time)
        cross_column = jnp.broadcast_to(cross_scale, (channels, channels)).T
        f_one[...] = cross_column * own_scale * time_scale
        centre_scale = jnp.where(wrap, own_scale, cross_scale)
        f_two[...] = jnp.broadcast_to(centre_scale, (channels, channels)).T * next_scale * time_scale
        for copy in (bins_zero, bins_one):
            copy.wait_recv()
        t_fwd[...] = bins[0].astype(F32).T
        t_rev[...] = b_cross[...].astype(F32)

        @pl.when(helper)
        def _():
            t_two[...] = b_near[...].astype(F32).T

        @pl.when(holder & (q != 0))
        def _():
            t_two[...] = b_near[...].astype(F32)

        @pl.when(holder & (q == 0))
        def _():
            t_two[...] = bins[1].astype(F32)

    after = None
    for i in range(2):
        rows = cross_rows(base + i * size)
        cross(i, 1).wait_recv()
        forward(i, base).start()
        spread_centre(centres.at[0], base + i * size, size, count)
        advance(i, centres.at[0, rows], near_c, after)
        if i == 0:
            tables()
        late = pl.ds(i * size, size)
        after = (f_one.at[rows], ((t_fwd.at[rows], acc_fwd), (t_rev.at[late], acc_rev)))

    @pl.when(wrap)
    def _():
        spread_centre(centres.at[1], 0, channels, count)

    chosen = jnp.where(wrap, 1, 0)
    to_above.wait_recv()
    spread_near(nbuf, near_n)
    for i in range(4):
        if i < rounds:
            pl.semaphore_wait(known.at[i], len(beside_us))
            if i + 1 < rounds:
                tell(i + 1)
        start = (base if i < 2 else other_base) + (i % 2) * size
        rows = cross_rows(start)
        if i >= 2:
            forward(i - 2, base).wait_recv()
            spread_centre(centres.at[0], start, size, count)
        advance(i, centres.at[chosen, rows], near_n, after)
        after = (f_two.at[rows], ((t_two.at[rows], acc_two),))
    for i in range(4, rounds):
        pl.semaphore_wait(known.at[i], len(beside_us))
        if i + 1 < rounds:
            tell(i + 1)
    advance(4, None, None, after)

    flip = lax.broadcasted_iota(jnp.int32, (ROWS, ROWS), 0) + lax.broadcasted_iota(jnp.int32, (ROWS, ROWS), 1)
    flip = jnp.where(flip == 2 * MAX_LAG, 1.0, 0.0).astype(F32)
    two = acc_two[...]
    ahead = acc_fwd[...] + jnp.where(holder, 0.0, two)
    back = acc_rev[...] + jnp.where(holder, two, 0.0)
    turned = lax.dot_general(
        back, flip, (((1,), (0,)), ((), ())), precision=lax.Precision.HIGHEST, preferred_element_type=F32
    )
    pair_total = ROUNDS * n_chan * channels * channels // NB
    part[...] = jnp.zeros_like(part)
    part[:, :ROWS] = (ahead + turned) * (1.0 / math.sqrt(pair_total))

    owned = part.shape[0] // n_chan
    first = []
    for k in range(1, n_chan):
        peer = lax.rem(chan + k, n_chan)
        src = part.at[pl.ds(pl.multiple_of(peer * owned, owned), owned)]
        copy = send(src, arrived.at[k - 1], r_send.at[k - 1], r_recv.at[k - 1], (peer, seg))
        copy.start()
        first.append(copy)
    running = part[pl.ds(pl.multiple_of(chan * owned, owned), owned), :]
    for k, copy in enumerate(first):
        copy.wait_recv()
        running = running + arrived[k]
    mine[...] = running
    others[seg] = running
    second = []
    for k in range(1, n_seg):
        copy = send(mine, others.at[seg], s_send.at[k], s_recv.at[k], (chan, lax.rem(seg + k, n_seg)))
        copy.start()
        second.append(copy)
    for copy in second:
        copy.wait_recv()
    sums = others[0]
    for s in range(1, n_seg):
        sums = sums + others[s]
    o_ref[...] = sums.T[:LAGS, :]

    for copy in e_copies + first + second:
        copy.wait_send()
    for i in range(2):
        forward(i, base).wait_send()

    @pl.when(holder)
    def _():
        for copy in from_holder:
            copy.wait_send()

        @pl.when(q != 0)
        def _():
            to_below.wait_send()

    @pl.when(helper)
    def _():
        for i in range(2):
            cross(i, 1).wait_send()
            cross(i, 0).wait_send()

        @pl.when(q == 0)
        def _():
            to_wrap.wait_send()


def local(traces, pair_bins):
    channels, length = traces.shape
    n_chan, n_seg = lax.axis_size("chan"), lax.axis_size("seg")
    size = channels // 4
    owned = NB // n_chan
    dma = pltpu.SemaphoreType.DMA
    block = pltpu.VMEM((channels, length), BF16)
    square = pltpu.VMEM((channels, channels), F32)
    wide = pltpu.VMEM((channels, length + 2 * NEAR * LANES), BF16)
    stacked = pltpu.VMEM((NB, ROWS), F32)
    return pl.pallas_call(
        functools.partial(kernel, n_chan, n_seg),
        out_shape=jax.ShapeDtypeStruct((LAGS, owned), F32),
        in_specs=[pl.BlockSpec(memory_space=pltpu.HBM)] * 2,
        out_specs=pl.BlockSpec(memory_space=pltpu.VMEM),
        scratch_shapes=[
            block,
            pltpu.VMEM((2, channels, channels), jnp.int32),
            block,
            pltpu.VMEM((2, channels, length + 2 * SPAN * LANES), BF16),
            block, wide, wide,
            pltpu.VMEM((2, COARSE, (FINE + 1) * size, channels), F32),
            dma((2,)),
            pltpu.VMEM((1, channels), F32),
            pltpu.VMEM((3, n_seg, 1, channels), F32),
            pltpu.VMEM((2, channels, channels), BF16),
            pltpu.VMEM((channels // 2, channels), BF16),
            pltpu.VMEM((channels, channels), BF16),
            square, pltpu.VMEM((channels // 2, channels), F32), square, square, square,
            stacked, stacked, stacked,
            pltpu.VMEM((channels, LANES), F32),
            pltpu.VMEM((NB, LANES), F32),
            pltpu.VMEM((n_chan - 1, owned, LANES), F32),
            pltpu.VMEM((owned, LANES), F32),
            pltpu.VMEM((n_seg, owned, LANES), F32),
            dma((4, n_seg)), dma((3, n_seg)), dma((2,)), dma((2, 2)), dma((2,)), dma((2,)), dma((2,)),
            dma((2,)), dma((1,)), dma((4,)), dma((2,)),
            dma((n_chan - 1,)), dma((n_chan - 1,)), dma((n_seg,)), dma((n_seg,)),
            pltpu.SemaphoreType.REGULAR((n_chan // 4,)),
        ],
        compiler_params=pltpu.CompilerParams(
            collective_id=0, has_side_effects=True, vmem_limit_bytes=63 * 1024 * 1024
        ),
    )(traces, pair_bins)


def solution(mesh):
    in_specs = (P("chan", "seg"), P(None, "chan", None))
    out_specs = P(None, "chan")
    return jax.shard_map(local, mesh=mesh, in_specs=in_specs, out_specs=out_specs, check_vma=False)
```

```python
import functools
import math

import jax
import jax.numpy as jnp
from jax import lax
from jax.experimental import pallas as pl
from jax.experimental.pallas import tpu as pltpu
from jax.sharding import PartitionSpec as P

MAX_LAG = 32
NB = 256
ROUNDS = 2
LAGS = 2 * MAX_LAG + 1
EPSILON = 1e-06

FINE = 8
COARSE = 2 * MAX_LAG // FINE
LANES = 128
ROWS = 80
TILE = 16
GROUP = 16
MESH = pl.DeviceIdType.MESH
CONTRACT = (((1,), (1,)), ((), ()))
F32, BF16 = jnp.float32, jnp.bfloat16

NEAR = MAX_LAG - FINE
SPAN = FINE


def dot(left, right):
    return lax.dot_general(left, right, CONTRACT, preferred_element_type=F32)


def lanes(rows):
    return lax.broadcasted_iota(jnp.int32, (rows, LANES), 1)


def columns_first(cols):
    count = len(cols)
    lane = lanes(cols[0].shape[0])
    step = 1
    while step < count:
        bit = (lane & step) != 0
        done = list(cols)
        for u in range(count):
            if not u & step:
                low, high = cols[u], cols[u + step]
                done[u] = jnp.where(bit, pltpu.roll(high, step, 1), low)
                done[u + step] = jnp.where(bit, high, pltpu.roll(low, LANES - step, 1))
        cols = done
        step *= 2
    return cols


def later(col, count):
    lane = lanes(col.shape[0])
    inner = pltpu.roll(col, LANES - count, 1)
    outer = jnp.where(lane < LANES - 1, pltpu.roll(col, LANES - count - 1, 1), 0.0)
    return jnp.where(lane < LANES - count, inner, outer)


def earlier(col, count):
    lane = lanes(col.shape[0])
    inner = pltpu.roll(col, count, 1)
    outer = jnp.where(lane > 0, pltpu.roll(col, count + 1, 1), 0.0)
    return jnp.where(lane >= count, inner, outer)


def at(column):
    return slice(column * LANES, (column + 1) * LANES)


def beside(load, store, count, low, high):
    for i in range(count):
        col = None
        for c in range(i + count, count + high, count):
            col = later(load(i) if col is None else col, count)
            store(c, col)
        col = None
        for c in range(i - count, -low - 1, -count):
            col = earlier(load(i) if col is None else col, count)
            store(c, col)


def spread_near(source, wide):
    rows, length = source.shape
    count = length // LANES

    @pl.loop(0, rows // TILE)
    def _(g):
        here = pl.ds(pl.multiple_of(g * TILE, TILE), TILE)
        wide[here, NEAR * LANES : NEAR * LANES + length] = source[here, :]

        def store(c, col):
            wide[here, at(NEAR + c)] = col.astype(BF16)

        beside(lambda i: source[here, at(i)].astype(F32), store, count, NEAR, NEAR)


def spread_centre(block, start, rows, count):
    @pl.loop(0, rows // TILE)
    def _(g):
        here = pl.ds(pl.multiple_of(start + g * TILE, TILE), TILE)

        def store(c, col):
            block[here, at(SPAN + c)] = col.astype(BF16)

        beside(lambda i: block[here, at(SPAN + i)].astype(F32), store, count, SPAN, SPAN)


def correlate(centre, near, raw, piece):
    rows, span = centre.shape
    length = span - 2 * SPAN * LANES
    pair = 2
    steps = FINE + 1 if piece == COARSE // pair - 1 else FINE
    first = 0 if piece < COARSE // pair // 2 else SPAN
    left = [centre[:, (first + f) * LANES : (first + f) * LANES + length] for f in range(steps)]
    right = []
    for k in range(pair * piece, pair * piece + pair):
        column = NEAR - FINE * (k - COARSE // 2) - (FINE if k < COARSE // 2 else 0)
        right.append(near[:, column * LANES : column * LANES + length])
    out = dot(jnp.concatenate(left, 0), jnp.concatenate(right, 0))
    width = near.shape[0]
    for k in range(pair):
        raw[pair * piece + k, : steps * rows, :] = out[:, k * width : (k + 1) * width]


def bin_rows(raw, rows, start, factors, table, acc):
    width = factors.shape[1]
    ids = lax.broadcasted_iota(jnp.int32, (NB, width), 0).astype(F32).astype(BF16)
    one, none = jnp.asarray(1, BF16), jnp.asarray(0, BF16)

    @pl.loop(0, rows // GROUP)
    def _(g):
        lead = pl.multiple_of(g * GROUP, GROUP)
        here = pl.ds(pl.multiple_of(start + lead, GROUP), GROUP)
        factor, bins = factors[here, :], table[here, :].astype(BF16)
        last = raw[COARSE - 1, pl.ds(pl.multiple_of(FINE * rows + lead, GROUP), GROUP), :] * factor
        scores, hots = [], []
        for x in range(GROUP):
            each = jnp.broadcast_to(factor[x : x + 1, :], (FINE, width))
            pieces = [raw[k, pl.ds(lead + x, FINE, stride=rows), :] * each for k in range(COARSE)]
            edge = jnp.broadcast_to(last[x : x + 1, :], (FINE, width))
            scores.append(jnp.concatenate(pieces + [edge, edge], 0).astype(BF16))
            hit = jnp.broadcast_to(bins[x : x + 1, :], (NB, width)) == ids
            hots.append(jnp.where(hit, one, none))
        acc[...] += dot(jnp.concatenate(hots, 1), jnp.concatenate(scores, 1))


def kernel(
    n_chan, n_seg, x_ref, b_ref, o_ref,
    trace, bins, cbuf, centres, nbuf, near, raw, i_sem, e_out, e_in, b_out, b_cross, b_near,
    tabs, factors, accs, squares, part, arrived, mine, others,
    e_send, e_recv, c_sem, x_send, x_recv, w_send, w_recv, n_send, n_recv, b_send, b_recv, r_send, r_recv, s_send, s_recv, known,
):
    channels, length = trace.shape
    count = length // LANES
    half = channels // 2
    size = half // 2
    chan, seg = lax.axis_index("chan"), lax.axis_index("seg")
    loop = n_chan // 2
    side = chan // loop
    q = chan - side * loop
    parity = lax.rem(seg, 2)
    twin = seg + 1 - 2 * parity
    holder = parity == side
    helper = parity != side
    across = lax.rem(chan + loop, n_chan)
    above = side * loop + lax.rem(q + 1, loop)
    below = side * loop + lax.rem(q + loop - 1, loop)
    base = pl.multiple_of(half * jnp.where(holder, 1, 0), size)
    other_base = pl.multiple_of(half - base, size)
    wrap = (holder & (q == 0)) | (helper & (q == loop - 1))

    def send(src, dst, s_sem, r_sem, device):
        return pltpu.make_async_remote_copy(
            src_ref=src, dst_ref=dst, send_sem=s_sem, recv_sem=r_sem, device_id=device, device_id_type=MESH
        )

    bins_in = pltpu.make_async_copy(b_ref, bins, i_sem.at[0])
    trace_in = pltpu.make_async_copy(x_ref, trace, i_sem.at[1])
    trace_in.start()
    bins_in.start()
    xbuf = centres.at[0, :, pl.ds(SPAN * LANES, length)]
    own = centres.at[1, :, pl.ds(SPAN * LANES, length)]
    barrier = pltpu.get_barrier_semaphore()
    beside_us = [(across, seg), (above, seg), (below, seg)]
    peers = list(beside_us)
    for k in range(1, n_seg):
        to = lax.rem(seg + k, n_seg)
        peers += [(chan, to), (across, to), (above, to), (below, to)]
    for peer in peers:
        pl.semaphore_signal(barrier, inc=1, device_id=peer, device_id_type=MESH)

    bins_in.wait()
    b_out[...] = bins[...].astype(F32).astype(BF16)
    trace_in.wait()
    squares[...] = jnp.zeros_like(squares)

    @pl.loop(0, channels // TILE)
    def _(g):
        here = pl.ds(pl.multiple_of(g * TILE, TILE), TILE)
        cols = [trace[here, at(i)].astype(F32) for i in range(count)]
        total = jnp.square(cols[0])
        for col in cols[1:]:
            total += jnp.square(col)
        squares[here, :] = total
        for i, col in enumerate(columns_first(cols)):
            own[here, at(i)] = col.astype(BF16)

    own_energy = jnp.sum(squares[...].T, axis=0, keepdims=True)
    e_out[...] = own_energy
    e_in[0, seg] = own_energy
    accs[...] = jnp.zeros_like(accs)
    pl.semaphore_wait(barrier, len(peers))

    def tell(i):
        for peer in beside_us:
            pl.semaphore_signal(known.at[i], inc=1, device_id=peer, device_id_type=MESH)

    rounds = loop // 2
    tell(0)

    e_copies = []
    for k in range(1, n_seg):
        to = lax.rem(seg + k, n_seg)
        e_copies.append(send(e_out, e_in.at[0, seg], e_send.at[0, k], e_recv.at[0, k], (chan, to)))
    for k in range(n_seg):
        to = lax.rem(seg + k, n_seg)
        e_copies.append(send(e_out, e_in.at[1, seg], e_send.at[1, k], e_recv.at[1, k], (across, to)))
    for k in range(n_seg // 2):
        to = lax.rem(2 * k + side + seg - parity, n_seg)
        to_helper = lax.rem(2 * k + 1 - side + seg - parity, n_seg)
        e_copies.append(send(e_out, e_in.at[2, seg], e_send.at[2, k], e_recv.at[2, 2 * k + parity], (above, to)))
        e_copies.append(send(e_out, e_in.at[2, seg], e_send.at[3, k], e_recv.at[2, 2 * k + parity], (below, to_helper)))
    for copy in e_copies:
        copy.start()

    def cross_rows(start):
        return pl.ds(pl.multiple_of(start, size), size)

    def cross(i, to_holder):
        rows = cross_rows(i * size + (half if to_holder else 0))
        return send(own.at[rows], xbuf.at[rows], x_send.at[i, to_holder], x_recv.at[i], (across, seg if to_holder else twin))

    to_twin = send(own, cbuf, c_sem.at[0], c_sem.at[1], (chan, twin))
    to_above = send(own, nbuf, n_send.at[0], n_recv.at[0], (above, seg))
    to_below = send(own, nbuf, n_send.at[1], n_recv.at[0], (below, twin))
    to_wrap = send(own, nbuf, n_send.at[1], n_recv.at[0], (below, seg))
    bins_zero = send(b_out.at[0, pl.ds(0, half)], b_cross, b_send.at[0], b_recv.at[0], (across, seg))
    bins_half = send(b_out.at[0, pl.ds(half, half)], b_cross, b_send.at[1], b_recv.at[0], (across, twin))
    bins_one = send(b_out.at[1], b_near, b_send.at[2], b_recv.at[1], (across, twin))
    bins_below = send(b_out.at[1], b_near, b_send.at[3], b_recv.at[1], (below, twin))
    from_holder = (to_twin, to_above, bins_zero, bins_half, bins_one, bins_below)

    @pl.when(holder)
    def _():
        to_twin.start()
        for copy in (bins_zero, bins_half, bins_one, bins_below):
            copy.start()
        to_above.start()

        @pl.when(q != 0)
        def _():
            to_below.start()

        spread_near(own, near.at[0])

    @pl.when(helper)
    def _():
        for i in range(2):
            cross(i, 1).start()
            cross(i, 0).start()

        @pl.when(q == 0)
        def _():
            to_wrap.start()

        to_twin.wait_recv()
        spread_near(cbuf, near.at[0])

    def forward(i, start):
        rows = cross_rows(start + i * size)
        return send(xbuf.at[rows], xbuf.at[rows], w_send.at[i], w_recv.at[i], (chan, twin))

    def tables():
        for k in range(1, n_seg):
            send(e_out, e_in.at[0, 0], e_send.at[0, k], e_recv.at[0, k], (chan, seg)).wait_recv()
        for k in range(n_seg):
            send(e_out, e_in.at[1, 0], e_send.at[1, k], e_recv.at[1, k], (chan, seg)).wait_recv()
            send(e_out, e_in.at[2, 0], e_send.at[2, 0], e_recv.at[2, k], (chan, seg)).wait_recv()
        total_time = length * n_seg

        def scale(slot):
            energy = e_in[slot, 0]
            for s in range(1, n_seg):
                energy = energy + e_in[slot, s]
            return lax.rsqrt(energy * (1.0 / total_time) + EPSILON)

        own_scale, cross_scale, next_scale = scale(0), scale(1), scale(2)
        time_scale = 1.0 / math.sqrt(total_time)
        cross_column = jnp.broadcast_to(cross_scale, (channels, channels)).T
        factors[0] = cross_column * own_scale * time_scale
        centre_scale = jnp.where(wrap, own_scale, cross_scale)
        factors[1] = jnp.broadcast_to(centre_scale, (channels, channels)).T * next_scale * time_scale
        for copy in (bins_zero, bins_one):
            copy.wait_recv()
        tabs[0] = bins[0].astype(F32).T
        tabs[2, pl.ds(base, half), :] = b_cross[...].astype(F32)

        @pl.when(helper)
        def _():
            tabs[1] = b_near[...].astype(F32).T

        @pl.when(holder & (q != 0))
        def _():
            tabs[1] = b_near[...].astype(F32)

        @pl.when(holder & (q == 0))
        def _():
            tabs[1] = bins[1].astype(F32)

    @pl.when(wrap)
    def _():
        spread_centre(centres.at[1], 0, channels, count)

    def known_by(i):
        pl.semaphore_wait(known.at[i], len(beside_us))

        @pl.when(i + 1 < rounds)
        def _():
            tell(i + 1)

    @pl.loop(0, 6)
    def _(j):
        phase = jnp.where(j >= 2, 1, 0)
        start = jnp.where(j >= 4, other_base + (j - 4) * size, base + lax.rem(j, 2) * size)
        start = pl.multiple_of(start, size)

        @pl.when(j < 2)
        def _():
            cross(j, 1).wait_recv()
            forward(j, base).start()

        @pl.when(j >= 4)
        def _():
            forward(j - 4, base).wait_recv()

        @pl.when((j < 2) | (j >= 4))
        def _():
            spread_centre(centres.at[0], start, size, count)

        @pl.when(j == 2)
        def _():
            to_above.wait_recv()
            spread_near(nbuf, near.at[1])

        @pl.when((j >= 2) & (j < 2 + rounds))
        def _():
            known_by(j - 2)

        chosen = jnp.where(wrap, phase, 0)
        for p in range(COARSE // 2):
            correlate(centres.at[chosen, pl.ds(start, size)], near.at[phase], raw, p)

        @pl.when(j == 0)
        def _():
            tables()

        bin_rows(raw, size, start, factors.at[phase], tabs.at[phase], accs.at[phase])

        @pl.when(j < 2)
        def _():
            bin_rows(raw, size, start, factors.at[0], tabs.at[2], accs.at[2])

    for i in range(4, rounds):
        known_by(i)

    flip = lax.broadcasted_iota(jnp.int32, (ROWS, ROWS), 0) + lax.broadcasted_iota(jnp.int32, (ROWS, ROWS), 1)
    flip = jnp.where(flip == 2 * MAX_LAG, 1.0, 0.0).astype(F32)
    two = accs[1]
    ahead = accs[0] + jnp.where(holder, 0.0, two)
    back = accs[2] + jnp.where(holder, two, 0.0)
    turned = lax.dot_general(
        back, flip, (((1,), (0,)), ((), ())), precision=lax.Precision.HIGHEST, preferred_element_type=F32
    )
    pair_total = ROUNDS * n_chan * channels * channels // NB
    part[...] = jnp.zeros_like(part)
    part[:, :ROWS] = (ahead + turned) * (1.0 / math.sqrt(pair_total))

    owned = part.shape[0] // n_chan
    first = []
    for k in range(1, n_chan):
        peer = lax.rem(chan + k, n_chan)
        src = part.at[pl.ds(pl.multiple_of(peer * owned, owned), owned)]
        copy = send(src, arrived.at[k - 1], r_send.at[k - 1], r_recv.at[k - 1], (peer, seg))
        copy.start()
        first.append(copy)
    running = part[pl.ds(pl.multiple_of(chan * owned, owned), owned), :]
    for k, copy in enumerate(first):
        copy.wait_recv()
        running = running + arrived[k]
    mine[...] = running
    others[seg] = running
    second = []
    for k in range(1, n_seg):
        copy = send(mine, others.at[seg], s_send.at[k], s_recv.at[k], (chan, lax.rem(seg + k, n_seg)))
        copy.start()
        second.append(copy)
    for copy in second:
        copy.wait_recv()
    sums = others[0]
    for s in range(1, n_seg):
        sums = sums + others[s]
    o_ref[...] = sums.T[:LAGS, :]

    for copy in e_copies + first + second:
        copy.wait_send()
    for i in range(2):
        forward(i, base).wait_send()

    @pl.when(holder)
    def _():
        for copy in from_holder:
            copy.wait_send()

        @pl.when(q != 0)
        def _():
            to_below.wait_send()

    @pl.when(helper)
    def _():
        for i in range(2):
            cross(i, 1).wait_send()
            cross(i, 0).wait_send()

        @pl.when(q == 0)
        def _():
            to_wrap.wait_send()


def local(traces, pair_bins):
    channels, length = traces.shape
    n_chan, n_seg = lax.axis_size("chan"), lax.axis_size("seg")
    size = channels // 4
    owned = NB // n_chan
    dma = pltpu.SemaphoreType.DMA
    block = pltpu.VMEM((channels, length), BF16)
    return pl.pallas_call(
        functools.partial(kernel, n_chan, n_seg),
        out_shape=jax.ShapeDtypeStruct((LAGS, owned), F32),
        in_specs=[pl.BlockSpec(memory_space=pltpu.HBM)] * 2,
        out_specs=pl.BlockSpec(memory_space=pltpu.VMEM),
        scratch_shapes=[
            block,
            pltpu.VMEM((2, channels, channels), jnp.int32),
            block,
            pltpu.VMEM((2, channels, length + 2 * SPAN * LANES), BF16),
            block,
            pltpu.VMEM((2, channels, length + 2 * NEAR * LANES), BF16),
            pltpu.VMEM((COARSE, (FINE + 1) * size, channels), F32),
            dma((2,)),
            pltpu.VMEM((1, channels), F32),
            pltpu.VMEM((3, n_seg, 1, channels), F32),
            pltpu.VMEM((2, channels, channels), BF16),
            pltpu.VMEM((channels // 2, channels), BF16),
            pltpu.VMEM((channels, channels), BF16),
            pltpu.VMEM((3, channels, channels), F32),
            pltpu.VMEM((2, channels, channels), F32),
            pltpu.VMEM((3, NB, ROWS), F32),
            pltpu.VMEM((channels, LANES), F32),
            pltpu.VMEM((NB, LANES), F32),
            pltpu.VMEM((n_chan - 1, owned, LANES), F32),
            pltpu.VMEM((owned, LANES), F32),
            pltpu.VMEM((n_seg, owned, LANES), F32),
            dma((4, n_seg)), dma((3, n_seg)), dma((2,)), dma((2, 2)), dma((2,)), dma((2,)), dma((2,)),
            dma((2,)), dma((1,)), dma((4,)), dma((2,)),
            dma((n_chan - 1,)), dma((n_chan - 1,)), dma((n_seg,)), dma((n_seg,)),
            pltpu.SemaphoreType.REGULAR((n_chan // 4,)),
        ],
        compiler_params=pltpu.CompilerParams(
            collective_id=0, has_side_effects=True, vmem_limit_bytes=63 * 1024 * 1024
        ),
    )(traces, pair_bins)


def solution(mesh):
    in_specs = (P("chan", "seg"), P(None, "chan", None))
    out_specs = P(None, "chan")
    return jax.shard_map(local, mesh=mesh, in_specs=in_specs, out_specs=out_specs, check_vma=False)
```
